512 devices in a mesh: loop: 32 (over x, z_lo, core), grp: 16 (over z_hi, y).
Axes of the slice: x: 4, y: 4, z: 16 (z_hi: 4, z_lo: 4; z = z_hi * 4 + z_lo), core: 2. Of those that a mesh axis runs over, the one named last changes fastest.
Arguments:
- adjacency_tiles: bfloat16 [65536, 128, 128], P(('loop', 'grp')), may hold values from -0.046875 to 0.046875
- row_block: int32 [65536], P(('loop', 'grp')), may hold values from 0 to 31
- column_block: int32 [65536], P(('loop', 'grp')), may hold values from 0 to 15
- features: bfloat16 [65536, 256], P(('loop', 'grp')), may hold values from -6 to 6
- weight: bfloat16 [256, 256], replicated, may hold values from -0.375 to 0.375
- out_bias: float32 [256], replicated, may hold values from -3 to 3
Outputs:
- result: bfloat16 [65536, 256], P(('loop', 'grp'))
The draws below stay inside these ranges and needn't reach their ends.
All inputs are finite; a program needn't handle non-finite values.
Results may differ from the reference program's by a relative error of at most 0.0046.
Values may be sent and summed in bfloat16 or wider, within the bound.
No kernel may reach another device: no remote copies, remote signals or barrier semaphores. Data moves between devices by JAX's collectives and lax.ppermute only.
A program may use at most 128 MiB of HBM per device.

```python
import math
import jax
import jax.numpy as jnp
import numpy as np
from jax import lax

TILE = 128
F = 256
TILES_DEV = 128
NODES = 65536
TILES = 65536
N_LOOP = 32
N_GRP = 16


def touch_ends(array, own_key, least, high):
    dims = array.shape
    spot = [jax.random.randint(jax.random.fold_in(own_key, axis), (), 0, dims[axis]) for axis in range(len(dims))]
    array = array.at[tuple(spot)].set(least)
    longest = dims.index(max(dims))
    spot[longest] = (spot[longest] + 1) % dims[longest]
    return array.at[tuple(spot)].set(high)


def shard_levels(rng, dims, cuts, low, largest):
    gain, own = 1.0, jax.random.fold_in(rng, 6)
    for position, parts in cuts:
        steps = jnp.exp(jax.random.uniform(jax.random.fold_in(own, position), (parts,), jnp.float32, low / len(cuts), largest / len(cuts)))
        gain = gain * jnp.repeat(steps, dims[position] // parts).reshape([-1 if axis == position else 1 for axis in range(len(dims))])
    return gain


def rank_table(count, slope):
    portions = [(1 << 20) // math.isqrt(grade ** slope) + 1 for grade in range(1, count + 1)]
    spread = 1 + sum(portions) // (1 << 30)
    return np.cumsum(np.array([max(1, weight // spread) for weight in portions]))


def skewed_ids(own_key, dims, amount, slope):
    table = rank_table(amount, slope)
    ticket = jax.random.randint(jax.random.fold_in(own_key, 1), dims, 0, int(table[amount - 1]))
    standing = jnp.searchsorted(jnp.asarray(table, jnp.int32), ticket, side="right")
    return jax.random.permutation(jax.random.fold_in(own_key, 2), amount)[standing].astype(jnp.int32)


def scatter_about(rng, dims, width, reach, split=(), kind=jnp.bfloat16):
    entries = jax.random.normal(rng, dims, jnp.float32) * width
    if len(split) > 0:
        entries = shard_levels(rng, dims, split, -0.22, 0.18) * entries
    return jnp.clip(entries, min=-reach, max=reach).astype(kind)


def setup_inputs(seed: int = 0) -> dict:
    splits = jax.random.split(jax.random.key(seed), 7)
    return {
        "adjacency_tiles": scatter_about(splits[0], (TILES, TILE, TILE), (TILE * TILES_DEV) ** -0.5, 0.046875, ((0, 512),)),
        "row_block": touch_ends(skewed_ids(splits[1], (TILES,), N_LOOP, 1), jax.random.fold_in(splits[1], 3), 0, N_LOOP - 1).astype(jnp.int32),
        "column_block": touch_ends(jax.random.randint(splits[2], (TILES,), 0, N_GRP), jax.random.fold_in(splits[2], 1), 0, N_GRP - 1).astype(jnp.int32),
        "features": scatter_about(splits[3], (NODES, F), 1.0, 6.0, ((0, 512),)),
        "weight": scatter_about(splits[4], (F, F), F ** -0.5, 0.375),
        "out_bias": scatter_about(splits[5], (F,), 0.5, 3.0, (), jnp.float32),
    }


def reference(adjacency_tiles, row_block, column_block, features, weight, out_bias):
    device_count = N_LOOP * N_GRP
    tiles_dev = adjacency_tiles.reshape(device_count, TILES_DEV, TILE, TILE)
    rows_dev = row_block.reshape(device_count, TILES_DEV)
    columns_dev = column_block.reshape(device_count, TILES_DEV)
    sections = features.reshape(N_LOOP, N_GRP, TILE, F)

    def one_device(aggregate, device_index):
        loop_index = device_index // N_GRP
        group_index = device_index % N_GRP
        section_blocks = lax.dynamic_index_in_dim(sections, loop_index, 0, keepdims=False)
        picked = jnp.take(section_blocks, columns_dev[device_index], axis=0)
        products = jnp.einsum('tij,tjf->tif', tiles_dev[device_index].astype(jnp.float32), picked.astype(jnp.float32))
        partial_value = jax.ops.segment_sum(products, rows_dev[device_index], num_segments=N_LOOP)
        current = lax.dynamic_index_in_dim(aggregate, group_index, 1, keepdims=False)
        aggregate = lax.dynamic_update_index_in_dim(aggregate, current + partial_value, group_index, 1)
        return aggregate, None

    start = jnp.zeros((N_LOOP, N_GRP, TILE, F), jnp.float32)
    aggregate, unused = lax.scan(one_device, start, jnp.arange(device_count, dtype=jnp.int32))
    aggregate = aggregate.reshape(N_LOOP * N_GRP * TILE, F).astype(jnp.bfloat16)
    mixed = jnp.dot(aggregate, weight, preferred_element_type=jnp.float32) + out_bias
    return jax.nn.relu(mixed).astype(jnp.bfloat16)
```

```python
import functools

import jax
import jax.numpy as jnp
from jax import lax
from jax.experimental import pallas as pl
from jax.experimental.pallas import tpu as pltpu
from jax.sharding import Mesh, PartitionSpec as P

F32 = jnp.float32
BF16 = jnp.bfloat16
GROUP = 32
VMEM_LIMIT = 20 << 20


def tile_kernel(group, core_ref, rows_ref, cols_ref, adj_ref, feat_ref, own_ref, other_ref, acc):
    step = pl.program_id(0)
    half = own_ref.shape[0]
    core = core_ref[0]

    @pl.when(step == 0)
    def _():
        acc[...] = jnp.zeros_like(acc)

    for k in range(group):
        t = step * group + k
        row = rows_ref[t]
        col = cols_ref[t]
        slot = ((row & 1) ^ core) * half + (row >> 1)
        block = (col & 3) * 4 + (col >> 2)
        acc[slot] += jnp.dot(adj_ref[k], feat_ref[block], preferred_element_type=F32)

    @pl.when(step == pl.num_programs(0) - 1)
    def _():
        own_ref[...] = acc[:half]
        other_ref[...] = acc[half:].astype(BF16)


def tile_products(core, rows, cols, tiles, section):
    count, side, _ = tiles.shape
    width = section.shape[2]
    half = 16
    return pl.pallas_call(
        functools.partial(tile_kernel, GROUP),
        out_shape=(
            jax.ShapeDtypeStruct((half, side, width), F32),
            jax.ShapeDtypeStruct((half, side, width), BF16),
        ),
        grid_spec=pltpu.PrefetchScalarGridSpec(
            num_scalar_prefetch=3,
            grid=(count // GROUP,),
            in_specs=[
                pl.BlockSpec((GROUP, side, side), lambda i, *_: (i, 0, 0)),
                pl.BlockSpec(memory_space=pltpu.VMEM),
            ],
            out_specs=(pl.BlockSpec(memory_space=pltpu.VMEM),) * 2,
            scratch_shapes=[pltpu.VMEM((2 * half, side, width), F32)],
        ),
        cost_estimate=pl.CostEstimate(
            flops=2 * count * side * side * width,
            bytes_accessed=tiles.size * 2,
            transcendentals=0,
        ),
        compiler_params=pltpu.CompilerParams(vmem_limit_bytes=VMEM_LIMIT),
        name="tile_products",
    )(core, rows, cols, tiles, section)


def gather_blocks(blocks, axis):
    n = lax.axis_size(axis)
    copies = jnp.broadcast_to(blocks[None], (n,) + blocks.shape)
    copies = copies.reshape((-1,) + blocks.shape[1:])
    return lax.all_to_all(copies, axis, 0, 0, tiled=True)


def sum_scatter(blocks, axis):
    n = lax.axis_size(axis)
    arrived = lax.all_to_all(blocks, axis, 0, 0, tiled=True)
    parts = arrived.reshape((n, -1) + blocks.shape[1:]).astype(F32)
    total = parts[0]
    for i in range(1, n):
        total = total + parts[i]
    return total


def on_device(adjacency_tiles, row_block, column_block, features, weight, out_bias):
    core = lax.axis_index("c")
    section = gather_blocks(gather_blocks(features[None], "zh"), "y")
    own, other = tile_products(
        core.reshape(1).astype(jnp.int32), row_block, column_block, adjacency_tiles, section
    )
    received = lax.ppermute(other, "c", [(0, 1), (1, 0)])
    chip = (own + received.astype(F32)).astype(BF16)
    plane = sum_scatter(chip, "x").astype(BF16)
    aggregate = sum_scatter(plane, "zl")[0].astype(BF16)
    mixed = jnp.dot(aggregate, weight, preferred_element_type=F32) + out_bias
    return jax.nn.relu(mixed).astype(BF16)


def solution(mesh):
    fine = Mesh(mesh.devices.reshape(4, 4, 2, 4, 4), ("x", "zl", "c", "zh", "y"))
    every = ("x", "zl", "c", "zh", "y")
    in_specs = (P(every, None, None), P(every), P(every), P(every, None), P(), P())
    return jax.shard_map(
        on_device, mesh=fine, in_specs=in_specs, out_specs=P(every, None), check_vma=False
    )
```

```python
import functools

import jax
import jax.numpy as jnp
from jax import lax
from jax.experimental import pallas as pl
from jax.experimental.pallas import tpu as pltpu
from jax.sharding import Mesh, PartitionSpec as P

F32 = jnp.float32
BF16 = jnp.bfloat16
GROUP = 32
VMEM_LIMIT = 20 << 20


def tile_kernel(
    place_ref, rows_ref, cols_ref, adj_hbm, f0, f1, f2, f3, own_ref, other_ref, acc, feat, adj, sems
):
    half = own_ref.shape[0]
    count = adj.shape[0]
    groups = count // GROUP
    x = place_ref[0]
    core = place_ref[1]
    y = place_ref[2]

    def fetch(g):
        part = pl.ds(g * GROUP, GROUP)
        return pltpu.make_async_copy(adj_hbm.at[part], adj.at[part], sems.at[g])

    for g in range(groups):
        fetch(g).start()
    acc[...] = jnp.zeros_like(acc)
    for i, part in enumerate((f0, f1, f2, f3)):
        feat[4 * i : 4 * i + 4] = part[...]

    @pl.loop(0, groups)
    def _(g):
        fetch(g).wait()
        for k in range(GROUP):
            t = g * GROUP + k
            row = rows_ref[t]
            col = cols_ref[t]
            slot = ((row & 1) ^ core) * half + (((row >> 3) - x) & 3) * 4 + ((row >> 1) & 3)
            block = ((y - col) & 3) * 4 + (col >> 2)
            acc[slot] += jnp.dot(adj[t], feat[block], preferred_element_type=F32)

    own_ref[...] = acc[:half]
    other_ref[...] = acc[half:].astype(BF16)


def tile_products(place, rows, cols, tiles, parts):
    count, side, _ = tiles.shape
    width = parts[0].shape[2]
    half = 16
    vmem = pl.BlockSpec(memory_space=pltpu.VMEM)
    smem = pl.BlockSpec(memory_space=pltpu.SMEM)
    return pl.pallas_call(
        tile_kernel,
        out_shape=(
            jax.ShapeDtypeStruct((half, side, width), F32),
            jax.ShapeDtypeStruct((half, side, width), BF16),
        ),
        in_specs=[smem] * 3 + [pl.BlockSpec(memory_space=pltpu.HBM)] + [vmem] * 4,
        out_specs=(vmem, vmem),
        scratch_shapes=[
            pltpu.VMEM((2 * half, side, width), F32),
            pltpu.VMEM((16, side, width), BF16),
            pltpu.VMEM((count, side, side), BF16),
            pltpu.SemaphoreType.DMA((count // GROUP,)),
        ],
        cost_estimate=pl.CostEstimate(
            flops=2 * count * side * side * width,
            bytes_accessed=tiles.size * 2,
            transcendentals=0,
        ),
        compiler_params=pltpu.CompilerParams(vmem_limit_bytes=VMEM_LIMIT),
        name="tile_products",
    )(place, rows, cols, tiles, *parts)


def send(value, axis, distance):
    n = lax.axis_size(axis)
    return lax.ppermute(value, axis, [(i, (i + distance) % n) for i in range(n)])


def on_device(adjacency_tiles, row_block, column_block, features, weight, out_bias):
    place = jnp.stack([lax.axis_index(a) for a in ("x", "c", "y")]).astype(jnp.int32)
    column = lax.all_gather(features, "zh", axis=0)
    parts = [column] + [send(column, "y", d) for d in (1, 2, 3)]
    own, other = tile_products(place, row_block, column_block, adjacency_tiles, parts)
    received = send(other, "c", 1)
    chip = own + received.astype(F32)
    n = 4
    leaving = [chip[n * d : n * d + n].astype(BF16) for d in (1, 2, 3)]
    plane = chip[:n]
    for d in (1, 2, 3):
        plane = plane + send(leaving[d - 1], "x", d).astype(F32)
    zl = lax.axis_index("zl")
    arrived = lax.all_to_all(plane.astype(BF16), "zl", 0, 0, tiled=True).astype(F32)
    total = lax.optimization_barrier(lax.dynamic_index_in_dim(plane, zl, keepdims=False))
    for i in range(n):
        total = total + jnp.where(zl == i, 0.0, arrived[i])
    aggregate = total.astype(BF16)
    mixed = jnp.dot(aggregate, weight, preferred_element_type=F32) + out_bias
    return jax.nn.relu(mixed).astype(BF16)


def solution(mesh):
    fine = Mesh(mesh.devices.reshape(4, 4, 2, 4, 4), ("x", "zl", "c", "zh", "y"))
    every = ("x", "zl", "c", "zh", "y")
    in_specs = (P(every, None, None), P(every), P(every), P(every, None), P(), P())
    return jax.shard_map(
        on_device, mesh=fine, in_specs=in_specs, out_specs=P(every, None), check_vma=False
    )
```

```python
import jax
import jax.numpy as jnp
from jax import lax
from jax.experimental import pallas as pl
from jax.experimental.pallas import tpu as pltpu
from jax.sharding import Mesh, PartitionSpec as P

F32 = jnp.float32
BF16 = jnp.bfloat16
GROUP = 32
VMEM_LIMIT = 50 << 20


def tile_kernel(
    core_ref, rows_ref, cols_ref, adj_hbm, feat, own_ref, other_ref, acc, adj, sems
):
    half = own_ref.shape[0]
    count = adj.shape[0]
    groups = count // GROUP
    core = core_ref[0]

    def fetch(g):
        part = pl.ds(g * GROUP, GROUP)
        return pltpu.make_async_copy(adj_hbm.at[part], adj.at[part], sems.at[g])

    for g in range(groups):
        fetch(g).start()
    acc[...] = jnp.zeros_like(acc)

    @pl.loop(0, groups)
    def _(g):
        fetch(g).wait()
        for k in range(GROUP):
            t = g * GROUP + k
            row = rows_ref[t]
            col = cols_ref[t]
            slot = ((row & 1) ^ core) * half + (row >> 1)
            block = (col & 3) * 4 + (col >> 2)
            acc[slot] += jnp.dot(adj[t], feat[block], preferred_element_type=F32)

    own_ref[...] = acc[:half]
    other_ref[...] = acc[half:].astype(BF16)


def tile_products(core, rows, cols, tiles, section):
    count, side, _ = tiles.shape
    width = section.shape[2]
    half = 16
    vmem = pl.BlockSpec(memory_space=pltpu.VMEM)
    smem = pl.BlockSpec(memory_space=pltpu.SMEM)
    return pl.pallas_call(
        tile_kernel,
        out_shape=(
            jax.ShapeDtypeStruct((half, side, width), F32),
            jax.ShapeDtypeStruct((half, side, width), BF16),
        ),
        in_specs=[smem] * 3 + [pl.BlockSpec(memory_space=pltpu.HBM)] + [vmem],
        out_specs=(vmem, vmem),
        scratch_shapes=[
            pltpu.VMEM((2 * half, side, width), F32),
            pltpu.VMEM((count, side, side), BF16),
            pltpu.SemaphoreType.DMA((count // GROUP,)),
        ],
        cost_estimate=pl.CostEstimate(
            flops=2 * count * side * side * width,
            bytes_accessed=tiles.size * 2,
            transcendentals=0,
        ),
        compiler_params=pltpu.CompilerParams(vmem_limit_bytes=VMEM_LIMIT),
        name="tile_products",
    )(core, rows, cols, tiles, section)


def sum_scatter(blocks, axis):
    n = lax.axis_size(axis)
    me = lax.axis_index(axis)
    share = blocks.shape[0] // n
    arrived = lax.all_to_all(blocks.astype(BF16), axis, 0, 0, tiled=True).astype(F32)
    total = lax.optimization_barrier(lax.dynamic_slice_in_dim(blocks, me * share, share))
    for i in range(n):
        total = total + jnp.where(me == i, 0.0, arrived[i * share : (i + 1) * share])
    return total


def on_device(adjacency_tiles, row_block, column_block, features, weight, out_bias):
    core = lax.axis_index("c").reshape(1).astype(jnp.int32)
    column = lax.all_gather(features, "zh", axis=0)
    copies = jnp.broadcast_to(column[None], (4,) + column.shape).reshape(-1, *column.shape[1:])
    section = lax.all_to_all(copies, "y", 0, 0, tiled=True)
    own, other = tile_products(core, row_block, column_block, adjacency_tiles, section)
    received = lax.ppermute(other, "c", [(0, 1), (1, 0)])
    chip = own + received.astype(F32)
    plane = sum_scatter(chip, "x")
    aggregate = sum_scatter(plane, "zl")[0].astype(BF16)
    mixed = jnp.dot(aggregate, weight, preferred_element_type=F32) + out_bias
    return jax.nn.relu(mixed).astype(BF16)


def solution(mesh):
    fine = Mesh(mesh.devices.reshape(4, 4, 2, 4, 4), ("x", "zl", "c", "zh", "y"))
    every = ("x", "zl", "c", "zh", "y")
    in_specs = (P(every, None, None), P(every), P(every), P(every, None), P(), P())
    return jax.shard_map(
        on_device, mesh=fine, in_specs=in_specs, out_specs=P(every, None), check_vma=False
    )
```

```python
import jax
import jax.numpy as jnp
from jax import lax
from jax.experimental import pallas as pl
from jax.experimental.pallas import tpu as pltpu
from jax.sharding import Mesh, PartitionSpec as P

F32 = jnp.float32
BF16 = jnp.bfloat16
GROUP = 32
PIECE = 8
VMEM_LIMIT = 48 << 20


def tile_kernel(
    rows_ref, cols_ref, adj_hbm, feat, own_ref, other_ref, acc, adj, sems
):
    half = own_ref.shape[0]
    count = adj.shape[0]
    core = lax.axis_index("c")

    def fetch(i):
        part = pl.ds(i * PIECE, PIECE)
        return pltpu.make_async_copy(adj_hbm.at[part], adj.at[part], sems.at[i])

    for i in range(count // PIECE):
        fetch(i).start()
    acc[...] = jnp.zeros_like(acc)

    def run(first, size):
        for i in range(size // PIECE):
            fetch(first // PIECE + i).wait()
        for k in range(size):
            t = first + k
            row = rows_ref[t]
            col = cols_ref[t]
            to_x = row >> 3
            to_zl = (row >> 1) & 3
            chip = jnp.where((row & 1) == 0, 4 * to_x + to_zl, 4 * to_zl + to_x)
            slot = ((row & 1) ^ core) * half + chip
            block = (col & 3) * 4 + (col >> 2)
            acc[slot] += jnp.dot(adj[t], feat[block], preferred_element_type=F32)

    run(0, GROUP // 2)
    run(GROUP // 2, GROUP // 2)

    @pl.loop(1, count // GROUP)
    def _(g):
        run(g * GROUP, GROUP)

    own_ref[...] = acc[:half]
    other_ref[...] = acc[half:].astype(BF16)


def tile_products(rows, cols, tiles, section):
    count, side, _ = tiles.shape
    width = section.shape[2]
    half = 16
    vmem = pl.BlockSpec(memory_space=pltpu.VMEM)
    smem = pl.BlockSpec(memory_space=pltpu.SMEM)
    return pl.pallas_call(
        tile_kernel,
        out_shape=(
            jax.ShapeDtypeStruct((half, side, width), F32),
            jax.ShapeDtypeStruct((half, side, width), BF16),
        ),
        in_specs=[smem] * 2 + [pl.BlockSpec(memory_space=pltpu.HBM)] + [vmem],
        out_specs=(vmem, vmem),
        scratch_shapes=[
            pltpu.VMEM((2 * half, side, width), F32),
            pltpu.VMEM((count, side, side), BF16),
            pltpu.SemaphoreType.DMA((count // PIECE,)),
        ],
        cost_estimate=pl.CostEstimate(
            flops=2 * count * side * side * width,
            bytes_accessed=tiles.size * 2,
            transcendentals=0,
        ),
        compiler_params=pltpu.CompilerParams(vmem_limit_bytes=VMEM_LIMIT),
        name="tile_products",
    )(rows, cols, tiles, section)


def exchange(blocks, turned):
    along_x = [[(x * 4 + z) * 2 + turned for x in range(4)] for z in range(4)]
    along_zl = [[(x * 4 + z) * 2 + 1 - turned for z in range(4)] for x in range(4)]
    arrived = lax.all_to_all(
        blocks.astype(BF16),
        ("x", "zl", "c"),
        0,
        0,
        axis_index_groups=along_x + along_zl,
        tiled=True,
    )
    share = blocks.shape[0] // 4
    parts = arrived.astype(F32)
    total = parts[:share]
    for i in range(1, 4):
        total = total + parts[i * share : (i + 1) * share]
    return total


def on_device(adjacency_tiles, row_block, column_block, features, weight, out_bias):
    column = lax.all_gather(features, "zh", axis=0)
    copies = jnp.broadcast_to(column[None], (4,) + column.shape).reshape(-1, *column.shape[1:])
    section = lax.all_to_all(copies, "y", 0, 0, tiled=True)
    own, other = tile_products(row_block, column_block, adjacency_tiles, section)
    received = lax.ppermute(other, "c", [(0, 1), (1, 0)])
    chip = own + received.astype(F32)
    plane = exchange(chip, 0)
    aggregate = exchange(plane, 1)[0].astype(BF16)
    mixed = jnp.dot(aggregate, weight, preferred_element_type=F32) + out_bias
    return jax.nn.relu(mixed).astype(BF16)


def solution(mesh):
    fine = Mesh(mesh.devices.reshape(4, 4, 2, 4, 4), ("x", "zl", "c", "zh", "y"))
    every = ("x", "zl", "c", "zh", "y")
    in_specs = (P(every, None, None), P(every), P(every), P(every, None), P(), P())
    return jax.shard_map(
        on_device, mesh=fine, in_specs=in_specs, out_specs=P(every, None), check_vma=False
    )
```

```python
import jax
import jax.numpy as jnp
from jax import lax
from jax.experimental import pallas as pl
from jax.experimental.pallas import tpu as pltpu
from jax.sharding import Mesh, PartitionSpec as P

F32 = jnp.float32
BF16 = jnp.bfloat16
PIECES = ((0, 32), (32, 96))
VMEM_LIMIT = 48 << 20


def tile_kernel(
    rows_ref, cols_ref, adj_hbm, feat, own_ref, other_ref, acc, adj, sems
):
    half = own_ref.shape[0]
    core = lax.axis_index("c")

    def fetch(i):
        part = pl.ds(*PIECES[i])
        return pltpu.make_async_copy(adj_hbm.at[part], adj.at[part], sems.at[i])

    for i in range(len(PIECES)):
        fetch(i).start()
    acc[...] = jnp.zeros_like(acc)

    for i, (start, size) in enumerate(PIECES):
        fetch(i).wait()
        for t in range(start, start + size):
            row = rows_ref[t]
            col = cols_ref[t]
            to_x = row >> 3
            to_zl = (row >> 1) & 3
            chip = jnp.where((row & 1) == 0, 4 * to_x + to_zl, 4 * to_zl + to_x)
            slot = ((row & 1) ^ core) * half + chip
            block = (col & 3) * 4 + (col >> 2)
            acc[slot] += jnp.dot(adj[t], feat[block], preferred_element_type=F32)

    own_ref[...] = acc[:half]
    other_ref[...] = acc[half:].astype(BF16)


def tile_products(rows, cols, tiles, section):
    count, side, _ = tiles.shape
    width = section.shape[2]
    half = 16
    vmem = pl.BlockSpec(memory_space=pltpu.VMEM)
    smem = pl.BlockSpec(memory_space=pltpu.SMEM)
    return pl.pallas_call(
        tile_kernel,
        out_shape=(
            jax.ShapeDtypeStruct((half, side, width), F32),
            jax.ShapeDtypeStruct((half, side, width), BF16),
        ),
        in_specs=[smem] * 2 + [pl.BlockSpec(memory_space=pltpu.HBM)] + [vmem],
        out_specs=(vmem, vmem),
        scratch_shapes=[
            pltpu.VMEM((2 * half, side, width), F32),
            pltpu.VMEM((count, side, side), BF16),
            pltpu.SemaphoreType.DMA((len(PIECES),)),
        ],
        cost_estimate=pl.CostEstimate(
            flops=2 * count * side * side * width,
            bytes_accessed=tiles.size * 2,
            transcendentals=0,
        ),
        compiler_params=pltpu.CompilerParams(vmem_limit_bytes=VMEM_LIMIT),
        name="tile_products",
    )(rows, cols, tiles, section)


def exchange(blocks, turned):
    along_x = [[(x * 4 + z) * 2 + turned for x in range(4)] for z in range(4)]
    along_zl = [[(x * 4 + z) * 2 + 1 - turned for z in range(4)] for x in range(4)]
    arrived = lax.all_to_all(
        blocks.astype(BF16),
        ("x", "zl", "c"),
        0,
        0,
        axis_index_groups=along_x + along_zl,
        tiled=True,
    )
    share = blocks.shape[0] // 4
    total = arrived[:share].astype(F32)
    for i in range(1, 4):
        total = total + arrived[i * share : (i + 1) * share].astype(F32)
    return total


def on_device(adjacency_tiles, row_block, column_block, features, weight, out_bias):
    column = lax.all_gather(features, "zh", axis=0)
    copies = jnp.broadcast_to(column[None], (4,) + column.shape).reshape(-1, *column.shape[1:])
    section = lax.all_to_all(copies, "y", 0, 0, tiled=True)
    own, other = tile_products(row_block, column_block, adjacency_tiles, section)
    received = lax.ppermute(other, "c", [(0, 1), (1, 0)])
    chip = own + received.astype(F32)
    plane = exchange(chip, 0)
    aggregate = exchange(plane, 1)[0].astype(BF16)
    mixed = jnp.dot(aggregate, weight, preferred_element_type=F32) + out_bias
    return jax.nn.relu(mixed).astype(BF16)


def solution(mesh):
    fine = Mesh(mesh.devices.reshape(4, 4, 2, 4, 4), ("x", "zl", "c", "zh", "y"))
    every = ("x", "zl", "c", "zh", "y")
    in_specs = (P(every, None, None), P(every), P(every), P(every, None), P(), P())
    return jax.shard_map(
        on_device, mesh=fine, in_specs=in_specs, out_specs=P(every, None), check_vma=False
    )
```
